128 devices in a mesh: dp: 64 (over z, x_lo, y, core), tensor: 2 (over x_hi).
Axes of the slice: x: 4 (x_hi: 2, x_lo: 2; x = x_hi * 2 + x_lo), y: 4, z: 4, core: 2. Of those that a mesh axis runs over, the one named last changes fastest.
Arguments:
- hidden_in: bfloat16 [32768, 1024], P('dp'), may hold values from -16 to 16
- segment_ids: int32 [32768], P('dp'), may hold values from 0 to 79, never falling along the last dimension, each value on 1 to 2048 neighbouring positions
- ln_one_gain: float32 [1024], replicated, may hold values from 0.25 to 1.75
- ln_one_bias: float32 [1024], replicated, may hold values from -1.75 to 1.75
- w_query: bfloat16 [1024, 1024], P(None, 'tensor'), may hold values from -0.1875 to 0.1875
- w_key: bfloat16 [1024, 1024], P(None, 'tensor'), may hold values from -0.1875 to 0.1875
- w_value: bfloat16 [1024, 1024], P(None, 'tensor'), may hold values from -0.1875 to 0.1875
- b_query: float32 [1024], P('tensor'), may hold values from -3 to 3
- b_value: float32 [1024], P('tensor'), may hold values from -3 to 3
- w_out: bfloat16 [1024, 1024], P('tensor'), may hold values from -0.75 to 0.75
- b_out: float32 [1024], replicated, may hold values from -1.75 to 1.75
- ln_two_gain: float32 [1024], replicated, may hold values from 0.25 to 1.75
- ln_two_bias: float32 [1024], replicated, may hold values from -1.75 to 1.75
- w_fc: bfloat16 [1024, 4096], P(None, 'tensor'), may hold values from -0.1875 to 0.1875
- b_fc: float32 [4096], P('tensor'), may hold values from -3 to 3
- w_proj: bfloat16 [4096, 1024], P('tensor'), may hold values from -0.09375 to 0.09375
- b_proj: float32 [1024], replicated, may hold values from -1.75 to 1.75
- cotangent: float32 [32768, 1024], P('dp'), may hold values from -16 to 16
Outputs:
- block_out: float32 [32768, 1024], P('dp')
- input_grad: float32 [32768, 1024], P('dp')
- grad_ln_one_gain: float32 [1024], replicated
- grad_ln_one_bias: float32 [1024], replicated
- grad_query: float32 [1024, 1024], P('dp', 'tensor')
- grad_key: float32 [1024, 1024], P('dp', 'tensor')
- grad_value: float32 [1024, 1024], P('dp', 'tensor')
- grad_b_query: float32 [1024], P('tensor')
- grad_b_value: float32 [1024], P('tensor')
- grad_w_out: float32 [1024, 1024], P('tensor', 'dp')
- grad_b_out: float32 [1024], replicated
- grad_ln_two_gain: float32 [1024], replicated
- grad_ln_two_bias: float32 [1024], replicated
- grad_fc: float32 [1024, 4096], P('dp', 'tensor')
- grad_b_fc: float32 [4096], P('tensor')
- grad_proj: float32 [4096, 1024], P('tensor', 'dp')
- grad_b_proj: float32 [1024], replicated
The draws below stay inside these ranges and needn't reach their ends.
All inputs are finite; a program needn't handle non-finite values.
Results may differ from the reference program's by a relative error of at most 0.012.
Values sent between devices are 32-bit elements; how exact they have to be, the bound alone decides.
A program may use at most 256 MiB of HBM per device.

```python
import math
import jax
import jax.numpy as jnp
import numpy as np
from jax import lax

D = 1024
HEADS = 16
HEAD_DIM = 64
FF = 4096
SEQ = 512
TOKENS = 32768


def raised(entries, stream_key, source, target, parts, factor):
    owner, partner = [(jnp.arange(entries.shape[position]) // (entries.shape[position] // parts)).reshape([-1 if axis == position else 1 for axis in range(entries.ndim)]) for position in (source, target)]
    chosen = jax.random.permutation(stream_key, parts)[partner]
    strong = (owner == chosen) | (owner == (partner + parts // 2) % parts)
    return jnp.where(strong, factor * entries, entries)


def level_of(stream_key, extent, shards, least, largest):
    def one(dim, blocks):
        heights = jax.random.uniform(jax.random.fold_in(jax.random.fold_in(stream_key, 6), dim), (blocks,), jnp.float32, least / len(shards), largest / len(shards))
        return jnp.repeat(jnp.exp(heights), extent[dim] // blocks).reshape((-1,) + (1,) * (len(extent) - dim - 1))

    loudness = one(*shards[0])
    for cut in shards[1:]:
        loudness = loudness * one(*cut)
    return loudness


def split_up(number_of, total, reach, lean):
    portions = [(1 << 20) // math.isqrt(standing ** lean) + 1 for standing in range(2, number_of + 1)]
    spare, counts = total - reach - (number_of - 1), [1] * (number_of - 1)
    while spare > 0:
        candidates = [i for i in range(number_of - 1) if counts[i] < reach]
        mass, budget = sum([portions[i] for i in candidates]), spare
        for i in candidates:
            more = min(reach - counts[i], max(1, budget * portions[i] // mass), spare)
            counts[i] = counts[i] + more
            spare = spare - more
    return np.array([reach] + counts)


def ragged_sizes(stream_key, amount, total, limit, skew):
    if amount == 2:
        one = jax.random.randint(stream_key, (), max(1, total - limit), min(limit, total - 1) + 1)
        return jnp.stack([one, total - one])
    tallies = jnp.asarray(split_up(amount, total, limit, skew), jnp.int32)
    twos = (amount - 1) // 2
    donor, receiver = tallies[1:1 + 2 * twos:2], tallies[2:2 + 2 * twos:2]
    margin = jnp.minimum(donor - 1, limit - receiver)
    moved = jax.random.randint(jax.random.fold_in(stream_key, 1), (twos,), 0, 1 << 20) % (margin + 1)
    tallies = tallies.at[1:1 + 2 * twos:2].set(donor - moved).at[2:2 + 2 * twos:2].set(receiver + moved)
    return tallies[jax.random.permutation(jax.random.fold_in(stream_key, 2), amount)]


def gaussian(stream_key, shape, spread, limit, split=(), kind=jnp.bfloat16):
    loudness = level_of(stream_key, shape, split, -0.22, 0.18) if split else 1.0
    drawn = jax.random.normal(stream_key, shape, jnp.float32) * spread * loudness
    return jnp.minimum(jnp.maximum(drawn, -limit), limit).astype(kind)


def gaussian_with(own_key, extent, width, reach, pieces, heavy, kind=jnp.bfloat16):
    array = width * jax.random.normal(own_key, extent, jnp.float32)
    if pieces:
        array = array * level_of(own_key, extent, pieces, -0.22, 0.18)
    return jnp.clip(raised(array, jax.random.fold_in(own_key, 3), *heavy), -reach, reach).astype(kind)


def setup_inputs(seed: int = 0) -> dict:
    arg_keys = jax.random.split(jax.random.key(seed), 19)
    return {
        "hidden_in": gaussian_with(arg_keys[0], (TOKENS, D), 1.0, 16.0, ((0, 64),), (0, 1, 64, 4.0)),
        "segment_ids": jnp.searchsorted(jnp.cumsum(ragged_sizes(arg_keys[1], TOKENS * 5 // (4 * SEQ), TOKENS, 4 * SEQ, 1)), jnp.arange(TOKENS), side="right").astype(jnp.int32),
        "ln_one_gain": jnp.clip(1.0 + 0.15 * jax.random.normal(arg_keys[2], (D,), jnp.float32), 0.25, 1.75),
        "ln_one_bias": gaussian(arg_keys[3], (D,), 0.3, 1.75, (), jnp.float32),
        "w_query": gaussian(arg_keys[4], (D, D), D ** -0.5, 0.1875, ((1, 2),)),
        "w_key": gaussian(arg_keys[5], (D, D), D ** -0.5, 0.1875, ((1, 2),)),
        "w_value": gaussian(arg_keys[6], (D, D), D ** -0.5, 0.1875, ((1, 2),)),
        "b_query": gaussian(arg_keys[7], (D,), 0.5, 3.0, ((0, 2),), jnp.float32),
        "b_value": gaussian(arg_keys[8], (D,), 0.5, 3.0, ((0, 2),), jnp.float32),
        "w_out": gaussian(arg_keys[9], (D, D), (D // 16) ** -0.5, 0.75, ((0, 2),)),
        "b_out": gaussian(arg_keys[10], (D,), 0.3, 1.75, (), jnp.float32),
        "ln_two_gain": jnp.clip(1.0 + 0.15 * jax.random.normal(arg_keys[11], (D,), jnp.float32), 0.25, 1.75),
        "ln_two_bias": gaussian(arg_keys[12], (D,), 0.3, 1.75, (), jnp.float32),
        "w_fc": gaussian(arg_keys[13], (D, FF), D ** -0.5, 0.1875, ((1, 2),)),
        "b_fc": gaussian(arg_keys[14], (FF,), 0.5, 3.0, ((0, 2),), jnp.float32),
        "w_proj": gaussian(arg_keys[15], (FF, D), FF ** -0.5, 0.09375, ((0, 2),)),
        "b_proj": gaussian(arg_keys[16], (D,), 0.3, 1.75, (), jnp.float32),
        "cotangent": gaussian_with(arg_keys[17], (TOKENS, D), 1.0, 16.0, ((0, 64),), (0, 1, 64, 4.0), jnp.float32),
    }


EPS = 1e-05
GELU_C = 0.7978845608028654
CUBIC = 0.044715

def layer_norm(values, gain, shift):
    centre = values - lax.optimization_barrier(jnp.mean(values, axis=-1, keepdims=True))
    inverse = lax.rsqrt(lax.optimization_barrier(jnp.mean(centre * centre, axis=-1, keepdims=True)) + EPS)
    normed = centre * inverse
    return (normed * gain + shift, normed, inverse)

def norm_backward(grad_out, normed, inverse, gain):
    scaled = grad_out * gain
    grad_rows = inverse * (scaled - lax.optimization_barrier(jnp.mean(scaled, axis=-1, keepdims=True)) - normed * lax.optimization_barrier(jnp.mean(scaled * normed, axis=-1, keepdims=True)))
    return (grad_rows, lax.optimization_barrier(jnp.sum(grad_out * normed, axis=0)), lax.optimization_barrier(jnp.sum(grad_out, axis=0)))

def gelu_parts(inner):
    tangent = jnp.tanh(GELU_C * (inner + CUBIC * inner * inner * inner))
    value = 0.5 * inner * (1.0 + tangent)
    slope = 0.5 * (1.0 + tangent) + 0.5 * inner * (1.0 - tangent * tangent) * GELU_C * (1.0 + 3.0 * CUBIC * inner * inner)
    return (value, slope)

def fdot(left, right):
    return jnp.dot(left, right, preferred_element_type=jnp.float32)

def one_sequence(hidden, segments, cot, params):
    ln_one_gain, ln_one_bias, w_query, w_key, w_value, b_query, b_value, w_out, b_out, ln_two_gain, ln_two_bias, w_fc, b_fc, w_proj, b_proj = params
    scale = 1.0 / HEAD_DIM ** 0.5
    inputs = hidden.astype(jnp.float32)
    first_f, normed_one, inverse_one = layer_norm(inputs, ln_one_gain, ln_one_bias)
    first_in = first_f.astype(jnp.bfloat16)
    query = (fdot(first_in, w_query) + b_query).astype(jnp.bfloat16)
    keys = fdot(first_in, w_key).astype(jnp.bfloat16)
    values = (fdot(first_in, w_value) + b_value).astype(jnp.bfloat16)
    query_h = query.reshape(SEQ, HEADS, HEAD_DIM).astype(jnp.float32)
    keys_h = keys.reshape(SEQ, HEADS, HEAD_DIM).astype(jnp.float32)
    values_h = values.reshape(SEQ, HEADS, HEAD_DIM).astype(jnp.float32)
    rows = lax.broadcasted_iota(jnp.int32, (SEQ, SEQ), 0)
    cols = lax.broadcasted_iota(jnp.int32, (SEQ, SEQ), 1)
    allowed = ((cols <= rows) & (segments[:, None] == segments[None, :]))[None]
    scores = jnp.einsum('qhd,khd->hqk', query_h, keys_h) * scale
    masked = jnp.where(allowed, scores, -1e+30)
    top = lax.optimization_barrier(jnp.max(masked, axis=-1, keepdims=True))
    log_total = top + jnp.log(lax.optimization_barrier(jnp.sum(jnp.exp(masked - top), axis=-1, keepdims=True)))
    probs_f = jnp.exp(masked - log_total)
    probs = probs_f.astype(jnp.bfloat16)
    attended = jnp.einsum('hqk,khd->qhd', probs.astype(jnp.float32), values_h).astype(jnp.bfloat16)
    attended_flat = attended.reshape(SEQ, D)
    middle = inputs + fdot(attended_flat, w_out) + b_out
    second_f, normed_two, inverse_two = layer_norm(middle, ln_two_gain, ln_two_bias)
    second_in = second_f.astype(jnp.bfloat16)
    inner = fdot(second_in, w_fc) + b_fc
    activated_f, slope = gelu_parts(inner)
    activated = activated_f.astype(jnp.bfloat16)
    block_out = middle + fdot(activated, w_proj) + b_proj
    top_grad = cot.astype(jnp.bfloat16)
    grad_b_proj = lax.optimization_barrier(jnp.sum(cot, axis=0))
    grad_proj = fdot(activated.T, top_grad)
    grad_inner = fdot(top_grad, w_proj.T) * slope
    grad_b_fc = lax.optimization_barrier(jnp.sum(grad_inner, axis=0))
    grad_inner_b = grad_inner.astype(jnp.bfloat16)
    grad_fc = fdot(second_in.T, grad_inner_b)
    grad_second = fdot(grad_inner_b, w_fc.T)
    rows_two, grad_ln_two_gain, grad_ln_two_bias = norm_backward(grad_second, normed_two, inverse_two, ln_two_gain)
    grad_middle = cot + rows_two
    grad_b_out = lax.optimization_barrier(jnp.sum(grad_middle, axis=0))
    middle_b = grad_middle.astype(jnp.bfloat16)
    grad_w_out = fdot(attended_flat.T, middle_b)
    grad_attended = fdot(middle_b, w_out.T).astype(jnp.bfloat16)
    grad_att_h = grad_attended.reshape(SEQ, HEADS, HEAD_DIM).astype(jnp.float32)
    grad_probs = jnp.einsum('qhd,khd->hqk', grad_att_h, values_h)
    delta = lax.optimization_barrier(jnp.sum(probs_f * grad_probs, axis=-1, keepdims=True))
    grad_scores = (probs_f * (grad_probs - delta) * scale).astype(jnp.bfloat16).astype(jnp.float32)
    grad_q = jnp.einsum('hqk,khd->qhd', grad_scores, keys_h).reshape(SEQ, D)
    grad_k = jnp.einsum('hqk,qhd->khd', grad_scores, query_h).reshape(SEQ, D)
    grad_v = jnp.einsum('hqk,qhd->khd', probs.astype(jnp.float32), grad_att_h).reshape(SEQ, D)
    grad_b_query = lax.optimization_barrier(jnp.sum(grad_q, axis=0))
    grad_b_value = lax.optimization_barrier(jnp.sum(grad_v, axis=0))
    grad_q_b = grad_q.astype(jnp.bfloat16)
    grad_k_b = grad_k.astype(jnp.bfloat16)
    grad_v_b = grad_v.astype(jnp.bfloat16)
    grad_query = fdot(first_in.T, grad_q_b)
    grad_key = fdot(first_in.T, grad_k_b)
    grad_value = fdot(first_in.T, grad_v_b)
    grad_first = fdot(grad_q_b, w_query.T) + fdot(grad_k_b, w_key.T) + fdot(grad_v_b, w_value.T)
    rows_one, grad_ln_one_gain, grad_ln_one_bias = norm_backward(grad_first, normed_one, inverse_one, ln_one_gain)
    input_grad = grad_middle + rows_one
    grads = (grad_ln_one_gain, grad_ln_one_bias, grad_query, grad_key, grad_value, grad_b_query, grad_b_value, grad_w_out, grad_b_out, grad_ln_two_gain, grad_ln_two_bias, grad_fc, grad_b_fc, grad_proj, grad_b_proj)
    return (block_out, input_grad, grads)

def reference(hidden_in, segment_ids, ln_one_gain, ln_one_bias, w_query, w_key, w_value, b_query, b_value, w_out, b_out, ln_two_gain, ln_two_bias, w_fc, b_fc, w_proj, b_proj, cotangent):
    params = (ln_one_gain, ln_one_bias, w_query, w_key, w_value, b_query, b_value, w_out, b_out, ln_two_gain, ln_two_bias, w_fc, b_fc, w_proj, b_proj)
    seq_total = TOKENS // SEQ
    hidden_seqs = hidden_in.reshape(seq_total, SEQ, D)
    segment_seqs = segment_ids.reshape(seq_total, SEQ)
    cot_seqs = cotangent.reshape(seq_total, SEQ, D)
    shapes = [(D,), (D,), (D, D), (D, D), (D, D), (D,), (D,), (D, D), (D,), (D,), (D,), (D, FF), (FF,), (FF, D), (D,)]
    start = tuple((jnp.zeros(shape, jnp.float32) for shape in shapes))

    def advance(carry, items):
        hidden, segments, cot = items
        block_out, input_grad, grads = one_sequence(hidden, segments, cot, params)
        return (tuple((total + piece for total, piece in zip(carry, grads))), (block_out, input_grad))
    totals, outputs = lax.scan(advance, start, (hidden_seqs, segment_seqs, cot_seqs))
    block_out = outputs[0].reshape(TOKENS, D)
    input_grad = outputs[1].reshape(TOKENS, D)
    return (block_out, input_grad, totals[0], totals[1], totals[2], totals[3], totals[4], totals[5], totals[6], totals[7], totals[8], totals[9], totals[10], totals[11], totals[12], totals[13], totals[14])
```

```python
import functools

import jax
import jax.numpy as jnp
from jax import lax
from jax.experimental import pallas as pl
from jax.experimental.pallas import tpu as pltpu
from jax.sharding import PartitionSpec as P

HEAD_DIM = 64
SEQ = 512


EPS = 1e-05
GELU_C = 0.7978845608028654
CUBIC = 0.044715

MESH = pl.DeviceIdType.MESH
IN_PLACE = pl.BlockSpec(memory_space=pl.ANY)
IN_VMEM = pl.BlockSpec(memory_space=pltpu.VMEM)


def place():
    dp = lax.axis_index("dp")
    return dict(z=dp // 16, x=(dp // 8) % 2, y=(dp // 2) % 4, c=dp % 2, t=lax.axis_index("tensor"))


def device(p, **change):
    q = dict(p, **change)
    return {"dp": q["z"] * 16 + q["x"] * 8 + q["y"] * 2 + q["c"], "tensor": q["t"]}


def neighbours(p):
    near = {"partner": device(p, t=1 - p["t"]), "core": device(p, c=1 - p["c"]), "x": device(p, x=1 - p["x"])}
    for axis in "yz":
        for step, name in ((1, "up"), (2, "far"), (3, "down")):
            near[f"{axis}_{name}"] = device(p, **{axis: (p[axis] + step) % 4})
    return near


def greet(peers):
    barrier = pltpu.get_barrier_semaphore()
    for peer in peers:
        pl.semaphore_signal(barrier, inc=1, device_id=peer, device_id_type=MESH)
    pl.semaphore_wait(barrier, len(peers))


def remote(src, dst, sems, i, to):
    return pltpu.make_async_remote_copy(
        src_ref=src,
        dst_ref=dst,
        send_sem=sems.at[0, i],
        recv_sem=sems.at[1, i],
        device_id=to,
        device_id_type=MESH,
    )


CORE, VIA, DIRECT, VIA2, DIRECT2, LAST, COPIES = 0, 8, 10, 14, 16, 20, 21
ORDER = (2, 1, 3, 0)


def scatter_scratch(width):
    return [
        pltpu.VMEM((4, 2, 4, 16, width), jnp.float32),
        pltpu.VMEM((4, 2, 4, 16, width), jnp.float32),
        pltpu.VMEM((2, 4, 16, width), jnp.float32),
        pltpu.VMEM((2, 2, 4, 16, width), jnp.float32),
        pltpu.VMEM((2, 16, width), jnp.float32),
        pltpu.VMEM((2, 2, 16, width), jnp.float32),
        pltpu.VMEM((16, width), jnp.float32),
        pltpu.SemaphoreType.DMA((2, COPIES)),
        pltpu.SemaphoreType.DMA((8,)),
    ]


class Scatter:
    def __init__(self, grads, out, first, p, near, scratch):
        self.grads, self.out, self.first, self.p, self.near = grads, out, first, p, near
        self.own, self.other, self.via, self.fin, self.via2, self.fin2, self.last, self.sems, self.local = scratch
        self.second = "z" if first == "y" else "y"
        self.copies, self.locals = {}, {}

    def go(self, i, src, dst, to):
        self.copies[i] = remote(src, dst, self.sems, i, self.near[to])
        self.copies[i].start()

    def block(self, k, h, core):
        at = (self.p[self.first] + k) % 4
        return self.grads.at[:, h, at, core] if self.first == "y" else self.grads.at[at, h, :, core]

    def start(self):
        for k in ORDER:
            for h in range(2):
                i = 2 * k + h
                self.go(CORE + i, self.block(k, h, 1 - self.p["c"]), self.other.at[k, h], "core")
                self.locals[i] = pltpu.make_async_copy(
                    self.block(k, h, self.p["c"]), self.own.at[k, h], self.local.at[i]
                )
                self.locals[i].start()

    def paired(self, k):
        up, down = self.first + "_up", self.first + "_down"
        for h in range(2):
            i = 2 * k + h
            self.copies[CORE + i].wait_recv()
            self.locals[i].wait()

            def body(s, carry, h=h):
                self.own[k, h, s] = self.own[k, h, s] + self.other[k, h, s]
                return carry

            lax.fori_loop(0, 4, body, 0)
            block = self.own.at[k, h]
            if k == 2:
                self.go(VIA + h, block, self.via.at[h], (up, down)[h])
            elif k == 1 and h == 1:
                self.go(DIRECT + 1, block, self.fin.at[0, 1], up)
            elif k == 3 and h == 0:
                self.go(DIRECT + 2, block, self.fin.at[1, 0], down)

    def relayed(self):
        for h, k, to, i in ((0, 1, "_up", DIRECT), (1, 3, "_down", DIRECT + 3)):
            self.copies[VIA + h].wait_recv()

            def body(s, carry, h=h, k=k):
                self.own[k, h, s] = self.own[k, h, s] + self.via[h, s]
                return carry

            lax.fori_loop(0, 4, body, 0)
            self.go(i, self.own.at[k, h], self.fin.at[h, h], self.first + to)

    def first_done(self):
        m = self.p[self.second]
        up, down = self.second + "_up", self.second + "_down"
        for i in range(4):
            self.copies[DIRECT + i].wait_recv()
        for k in ORDER:
            at = (m + k) % 4
            for h in range(2):
                self.own[0, h, at] = self.own[0, h, at] + self.fin[0, h, at] + self.fin[1, h, at]
                block = self.own.at[0, h, at]
                if k == 2:
                    self.go(VIA2 + h, block, self.via2.at[h], (up, down)[h])
                elif k == 1 and h == 1:
                    self.go(DIRECT2 + 1, block, self.fin2.at[0, 1], up)
                elif k == 3 and h == 0:
                    self.go(DIRECT2 + 2, block, self.fin2.at[1, 0], down)

    def relayed2(self):
        m = self.p[self.second]
        for h, k, to, i in ((0, 1, "_up", DIRECT2), (1, 3, "_down", DIRECT2 + 3)):
            at = (m + k) % 4
            self.copies[VIA2 + h].wait_recv()
            self.own[0, h, at] = self.own[0, h, at] + self.via2[h]
            self.go(i, self.own.at[0, h, at], self.fin2.at[h, h], self.second + to)

    def second_done(self):
        m, x = self.p[self.second], self.p["x"]
        for i in range(4):
            self.copies[DIRECT2 + i].wait_recv()
        for h in range(2):
            self.own[0, h, m] = self.own[0, h, m] + self.fin2[0, h] + self.fin2[1, h]
        self.go(LAST, self.own.at[0, 1 - x, m], self.last, "x")

    def finish(self):
        m, x = self.p[self.second], self.p["x"]
        self.copies[LAST].wait_recv()
        self.out[...] = self.own[0, x, m] + self.last[...]
        for copy in self.copies.values():
            copy.wait_send()


SCATTER_REFS = len(scatter_scratch(128))


def small_scratch(rows, both):
    return [
        pltpu.VMEM((both, 128), jnp.float32),
        pltpu.VMEM((3, rows, 128), jnp.float32),
        pltpu.VMEM((2, rows, 128), jnp.float32),
        pltpu.VMEM((4, rows, 128), jnp.float32),
        pltpu.VMEM((4, rows, 128), jnp.float32),
        pltpu.SemaphoreType.DMA((2, 9)),
    ]


SMALL_REFS = len(small_scratch(8, 8))


class SmallSums:
    def __init__(self, rows, out, p, near, scratch):
        self.rows, self.out, self.p, self.near = rows, out, p, near
        self.from_partner, self.held, self.pair, self.along_y, self.along_z, self.sems = scratch
        self.both = self.from_partner.shape[0]
        self.copies = []

    def go(self, i, src, dst, to):
        copy = remote(src, dst, self.sems, i, self.near[to])
        copy.start()
        self.copies.append(copy)

    def start(self):
        self.go(0, self.rows.at[pl.ds(0, self.both)], self.from_partner, "partner")

    def to_core(self):
        self.copies[0].wait_recv()
        self.held[0] = self.rows[...]
        self.held[0, pl.ds(0, self.both)] = self.rows[pl.ds(0, self.both)] + self.from_partner[...]
        self.go(1, self.held.at[0], self.pair.at[0], "core")

    def to_x(self):
        self.copies[1].wait_recv()
        self.held[1] = self.held[0] + self.pair[0]
        self.go(2, self.held.at[1], self.pair.at[1], "x")

    def ring(self, axis, line, first):
        for i, name in enumerate(("_up", "_far", "_down")):
            self.go(first + i, line.at[self.p[axis]], line.at[self.p[axis]], axis + name)

    def to_y(self):
        self.copies[2].wait_recv()
        self.along_y[self.p["y"]] = self.held[1] + self.pair[1]
        self.ring("y", self.along_y, 3)

    def to_z(self):
        for i in range(3, 6):
            self.copies[i].wait_recv()
        a = self.along_y
        self.along_z[self.p["z"]] = a[0] + a[1] + a[2] + a[3]
        self.ring("z", self.along_z, 6)

    def finish(self):
        for i in range(6, 9):
            self.copies[i].wait_recv()
        a = self.along_z
        self.out[...] = a[0] + a[1] + a[2] + a[3]
        for copy in self.copies:
            copy.wait_send()


def reduce_kernel(firsts, has_small, *refs):
    refs = list(refs)

    def take(count):
        taken, refs[:] = refs[:count], refs[count:]
        return taken

    (terms_ref,), grads = take(1), take(len(firsts))
    rows = take(1) if has_small else []
    (theirs_ref,), outs = take(1), take(len(firsts))
    sums = take(1) if has_small else []
    p = place()
    near = neighbours(p)
    swap_sems = take(1)[0]
    scatters = [Scatter(g, o, f, p, near, take(SCATTER_REFS)) for g, o, f in zip(grads, outs, firsts)]
    small = SmallSums(rows[0], sums[0], p, near, take(SMALL_REFS)) if has_small else None
    names = ["partner", "core", "x", "y_up", "y_down", "z_up", "z_down"]
    if has_small:
        names += ["y_far", "z_far"]
    greet([near[name] for name in names])
    if has_small:
        small.start()
    swap = remote(terms_ref, theirs_ref, swap_sems, 0, near["partner"])
    swap.start()
    for s in scatters:
        s.start()
    beside = ["to_core", "to_x", "to_y", "to_z"]
    for k in ORDER:
        for s in scatters:
            s.paired(k)
        if has_small:
            getattr(small, beside.pop(0))()
    for name in ("relayed", "first_done", "relayed2", "second_done", "finish"):
        for s in scatters:
            getattr(s, name)()
    if has_small:
        small.finish()
    swap.wait()


def exchange_and_reduce(terms, grads, firsts, collective_id, rows=None, both=0):
    f32 = jnp.float32
    args = [terms] + [g.reshape(4, 2, 4, 2, 16, g.shape[1]) for g in grads]
    in_specs = [IN_PLACE] * len(args)
    out_shape = [jax.ShapeDtypeStruct(terms.shape, f32)]
    out_shape += [jax.ShapeDtypeStruct((16, g.shape[1]), f32) for g in grads]
    out_specs = [IN_PLACE] + [IN_VMEM] * len(grads)
    scratch = [pltpu.SemaphoreType.DMA((2, 1))]
    for g in grads:
        scratch += scatter_scratch(g.shape[1])
    if rows is not None:
        args.append(rows)
        in_specs.append(IN_VMEM)
        out_shape.append(jax.ShapeDtypeStruct(rows.shape, f32))
        out_specs.append(IN_VMEM)
        scratch += small_scratch(rows.shape[0], both)
    return pl.pallas_call(
        functools.partial(reduce_kernel, firsts, rows is not None),
        out_shape=out_shape,
        in_specs=in_specs,
        out_specs=out_specs,
        scratch_shapes=scratch,
        compiler_params=pltpu.CompilerParams(
            collective_id=collective_id, has_side_effects=True, vmem_limit_bytes=60 * 1024 * 1024
        ),
    )(*args)


def from_partner(value):
    return lax.ppermute(value, "tensor", [(0, 1), (1, 0)])


def layer_norm(values, gain, shift):
    centre = values - jnp.mean(values, axis=-1, keepdims=True)
    inverse = lax.rsqrt(jnp.mean(centre * centre, axis=-1, keepdims=True) + EPS)
    normed = centre * inverse
    return (normed * gain + shift, normed, inverse)


def norm_backward(grad_out, normed, inverse, gain):
    scaled = grad_out * gain
    return inverse * (
        scaled
        - jnp.mean(scaled, axis=-1, keepdims=True)
        - normed * jnp.mean(scaled * normed, axis=-1, keepdims=True)
    )


def gelu_parts(inner):
    tangent = jnp.tanh(GELU_C * (inner + CUBIC * inner * inner * inner))
    value = 0.5 * inner * (1.0 + tangent)
    slope = 0.5 * (1.0 + tangent) + 0.5 * inner * (1.0 - tangent * tangent) * GELU_C * (
        1.0 + 3.0 * CUBIC * inner * inner
    )
    return (value, slope)


def fdot(left, right):
    return jnp.dot(left, right, preferred_element_type=jnp.float32)


def contract_rows(left, right):
    return jnp.einsum("ta,tb->ab", left, right, preferred_element_type=jnp.float32)


def contract_cols(left, right):
    return jnp.einsum("ta,ba->tb", left, right, preferred_element_type=jnp.float32)


def allowed_mask(segments):
    rows = lax.broadcasted_iota(jnp.int32, (SEQ, SEQ), 0)
    cols = lax.broadcasted_iota(jnp.int32, (SEQ, SEQ), 1)
    same = segments[:, :, None] == segments[:, None, :]
    return (same & (cols <= rows)[None])[:, None]


def masked_scores(query, keys, allowed):
    scale = 1.0 / HEAD_DIM**0.5
    scores = jnp.einsum("bqhd,bkhd->bhqk", query, keys, preferred_element_type=jnp.float32) * scale
    return jnp.where(allowed, scores, -1e30)


def attend_forward(query, keys, values, allowed):
    masked = masked_scores(query, keys, allowed)
    top = jnp.max(masked, axis=-1, keepdims=True)
    log_total = top + jnp.log(jnp.sum(jnp.exp(masked - top), axis=-1, keepdims=True))
    probs = jnp.exp(masked - log_total).astype(jnp.bfloat16)
    attended = jnp.einsum("bhqk,bkhd->bqhd", probs, values, preferred_element_type=jnp.float32)
    return (attended.astype(jnp.bfloat16), log_total)


def attend_backward(query, keys, values, allowed, log_total, grad_attended):
    scale = 1.0 / HEAD_DIM**0.5
    probs_f = jnp.exp(masked_scores(query, keys, allowed) - log_total)
    probs = probs_f.astype(jnp.bfloat16)
    grad_probs = jnp.einsum(
        "bqhd,bkhd->bhqk", grad_attended, values, preferred_element_type=jnp.float32
    )
    delta = jnp.sum(probs_f * grad_probs, axis=-1, keepdims=True)
    grad_scores = (probs_f * (grad_probs - delta) * scale).astype(jnp.bfloat16)
    grad_q = jnp.einsum("bhqk,bkhd->bqhd", grad_scores, keys, preferred_element_type=jnp.float32)
    grad_k = jnp.einsum("bhqk,bqhd->bkhd", grad_scores, query, preferred_element_type=jnp.float32)
    grad_v = jnp.einsum("bhqk,bqhd->bkhd", probs, grad_attended, preferred_element_type=jnp.float32)
    return (grad_q, grad_k, grad_v)


def on_device(
    hidden_in,
    segment_ids,
    ln_one_gain,
    ln_one_bias,
    w_query,
    w_key,
    w_value,
    b_query,
    b_value,
    w_out,
    b_out,
    ln_two_gain,
    ln_two_bias,
    w_fc,
    b_fc,
    w_proj,
    b_proj,
    cotangent,
):
    tok_rows = hidden_in.shape[0]
    seq_count = tok_rows // SEQ
    local_width = w_query.shape[1]
    local_heads = local_width // HEAD_DIM

    def split_heads(flat):
        return flat.reshape(seq_count, SEQ, local_heads, HEAD_DIM)

    inputs = hidden_in.astype(jnp.float32)
    first_f, normed_one, inverse_one = layer_norm(inputs, ln_one_gain, ln_one_bias)
    first_in = first_f.astype(jnp.bfloat16)
    query = split_heads((fdot(first_in, w_query) + b_query).astype(jnp.bfloat16))
    keys = split_heads(fdot(first_in, w_key).astype(jnp.bfloat16))
    values = split_heads((fdot(first_in, w_value) + b_value).astype(jnp.bfloat16))
    allowed = allowed_mask(segment_ids.reshape(seq_count, SEQ))
    attended, log_total = attend_forward(query, keys, values, allowed)
    attended_flat = attended.reshape(tok_rows, local_width)
    attn_terms = fdot(attended_flat, w_out)
    middle = inputs + (attn_terms + from_partner(attn_terms)) + b_out
    second_f, normed_two, inverse_two = layer_norm(middle, ln_two_gain, ln_two_bias)
    second_in = second_f.astype(jnp.bfloat16)
    inner = fdot(second_in, w_fc) + b_fc
    activated_f, slope = gelu_parts(inner)
    activated = activated_f.astype(jnp.bfloat16)
    top_grad = cotangent.astype(jnp.bfloat16)
    grad_b_proj = jnp.sum(cotangent, axis=0)
    grad_inner = contract_cols(top_grad, w_proj) * slope
    grad_b_fc = jnp.sum(grad_inner, axis=0)
    grad_inner_b = grad_inner.astype(jnp.bfloat16)
    grad_proj = contract_rows(top_grad, activated)
    grad_fc = contract_rows(second_in, grad_inner_b)
    second_terms = contract_cols(grad_inner_b, w_fc)
    second_theirs, proj_share, fc_share = exchange_and_reduce(
        second_terms, (grad_proj, grad_fc), ("y", "z"), 1
    )
    activated_later, second_theirs = lax.optimization_barrier((activated, second_theirs))
    mlp_terms = fdot(activated_later, w_proj)
    block_out = middle + (mlp_terms + from_partner(mlp_terms)) + b_proj
    grad_second = second_terms + second_theirs
    rows_two = norm_backward(grad_second, normed_two, inverse_two, ln_two_gain)
    grad_ln_two_gain = jnp.sum(grad_second * normed_two, axis=0)
    grad_ln_two_bias = jnp.sum(grad_second, axis=0)
    grad_middle = cotangent + rows_two
    grad_b_out = jnp.sum(grad_middle, axis=0)
    middle_b = grad_middle.astype(jnp.bfloat16)
    grad_w_out = contract_rows(middle_b, attended_flat)
    grad_attended = contract_cols(middle_b, w_out).astype(jnp.bfloat16)
    grad_q, grad_k, grad_v = attend_backward(
        query, keys, values, allowed, log_total, split_heads(grad_attended)
    )
    grad_q = grad_q.reshape(tok_rows, local_width)
    grad_k = grad_k.reshape(tok_rows, local_width)
    grad_v = grad_v.reshape(tok_rows, local_width)
    grad_b_query = jnp.sum(grad_q, axis=0)
    grad_b_value = jnp.sum(grad_v, axis=0)
    grad_q_b = grad_q.astype(jnp.bfloat16)
    grad_k_b = grad_k.astype(jnp.bfloat16)
    grad_v_b = grad_v.astype(jnp.bfloat16)
    grad_query = contract_rows(first_in, grad_q_b)
    grad_key = contract_rows(first_in, grad_k_b)
    grad_value = contract_rows(first_in, grad_v_b)
    first_terms = (
        contract_cols(grad_q_b, w_query)
        + contract_cols(grad_k_b, w_key)
        + contract_cols(grad_v_b, w_value)
    )
    small = (
        jnp.sum(first_terms * normed_one, axis=0),
        jnp.sum(first_terms, axis=0),
        grad_b_query,
        grad_b_value,
        grad_b_out,
        grad_ln_two_gain,
        grad_ln_two_bias,
        grad_b_fc,
        grad_b_proj,
    )
    rows = jnp.concatenate([part.reshape(-1, 128) for part in small], axis=0)
    both = (small[0].size + small[1].size) // 128
    first_theirs, query_share, key_share, value_share, out_share, sums = exchange_and_reduce(
        first_terms, (grad_query, grad_key, grad_value, grad_w_out), ("y", "y", "z", "z"), 2, rows, both
    )
    input_grad = grad_middle + norm_backward(first_terms + first_theirs, normed_one, inverse_one, ln_one_gain)
    totals, at = [], 0
    for part in small:
        count = part.size // 128
        totals.append(sums[at : at + count].reshape(-1))
        at += count
    return (
        block_out,
        input_grad,
        totals[0],
        totals[1],
        query_share,
        key_share,
        value_share,
        totals[2],
        totals[3],
        out_share.T,
        totals[4],
        totals[5],
        totals[6],
        fc_share,
        totals[7],
        proj_share.T,
        totals[8],
    )


def solution(mesh):
    in_specs = (
        P("dp", None),
        P("dp"),
        P(),
        P(),
        P(None, "tensor"),
        P(None, "tensor"),
        P(None, "tensor"),
        P("tensor"),
        P("tensor"),
        P("tensor", None),
        P(),
        P(),
        P(),
        P(None, "tensor"),
        P("tensor"),
        P("tensor", None),
        P(),
        P("dp", None),
    )
    out_specs = (
        P("dp", None),
        P("dp", None),
        P(),
        P(),
        P("dp", "tensor"),
        P("dp", "tensor"),
        P("dp", "tensor"),
        P("tensor"),
        P("tensor"),
        P("tensor", "dp"),
        P(),
        P(),
        P(),
        P("dp", "tensor"),
        P("tensor"),
        P("tensor", "dp"),
        P(),
    )
    return jax.shard_map(
        on_device, mesh=mesh, in_specs=in_specs, out_specs=out_specs, check_vma=False
    )
```

```python
import functools

import jax
import jax.numpy as jnp
from jax import lax
from jax.experimental import pallas as pl
from jax.experimental.pallas import tpu as pltpu
from jax.sharding import PartitionSpec as P

HEAD_DIM = 64
SEQ = 512


EPS = 1e-05
GELU_C = 0.7978845608028654
CUBIC = 0.044715

MESH = pl.DeviceIdType.MESH
IN_PLACE = pl.BlockSpec(memory_space=pl.ANY)
IN_VMEM = pl.BlockSpec(memory_space=pltpu.VMEM)


def place():
    dp = lax.axis_index("dp")
    return dict(z=dp // 16, x=(dp // 8) % 2, y=(dp // 2) % 4, c=dp % 2, t=lax.axis_index("tensor"))


def device(p, **change):
    q = dict(p, **change)
    return {"dp": q["z"] * 16 + q["x"] * 8 + q["y"] * 2 + q["c"], "tensor": q["t"]}


def neighbours(p):
    near = {"partner": device(p, t=1 - p["t"]), "core": device(p, c=1 - p["c"]), "x": device(p, x=1 - p["x"])}
    for axis in "yz":
        for step, name in ((1, "up"), (2, "far"), (3, "down")):
            near[f"{axis}_{name}"] = device(p, **{axis: (p[axis] + step) % 4})
    return near


def greet(peers):
    barrier = pltpu.get_barrier_semaphore()
    for peer in peers:
        pl.semaphore_signal(barrier, inc=1, device_id=peer, device_id_type=MESH)
    pl.semaphore_wait(barrier, len(peers))


def remote(src, dst, sems, i, to):
    return pltpu.make_async_remote_copy(
        src_ref=src,
        dst_ref=dst,
        send_sem=sems.at[0, i],
        recv_sem=sems.at[1, i],
        device_id=to,
        device_id_type=MESH,
    )


CORE, VIA, DIRECT, VIA2, DIRECT2, LAST, COPIES = 0, 8, 10, 14, 16, 20, 21
ORDER = (2, 1, 3, 0)


def scatter_scratch(width):
    return [
        pltpu.VMEM((4, 2, 4, 16, width), jnp.float32),
        pltpu.VMEM((4, 2, 4, 16, width), jnp.float32),
        pltpu.VMEM((2, 4, 16, width), jnp.float32),
        pltpu.VMEM((2, 2, 4, 16, width), jnp.float32),
        pltpu.VMEM((2, 16, width), jnp.float32),
        pltpu.VMEM((2, 2, 16, width), jnp.float32),
        pltpu.VMEM((16, width), jnp.float32),
        pltpu.SemaphoreType.DMA((2, COPIES)),
        pltpu.SemaphoreType.DMA((8,)),
    ]


class Scatter:
    def __init__(self, grads, out, first, p, near, scratch):
        self.grads, self.out, self.first, self.p, self.near = grads, out, first, p, near
        self.own, self.other, self.via, self.fin, self.via2, self.fin2, self.last, self.sems, self.local = scratch
        self.second = "z" if first == "y" else "y"
        self.copies, self.locals = {}, {}

    def go(self, i, src, dst, to):
        self.copies[i] = remote(src, dst, self.sems, i, self.near[to])
        self.copies[i].start()

    def block(self, k, h, core):
        at = (self.p[self.first] + k) % 4
        return self.grads.at[:, h, at, core] if self.first == "y" else self.grads.at[at, h, :, core]

    def start(self):
        for k in ORDER:
            for h in range(2):
                i = 2 * k + h
                self.go(CORE + i, self.block(k, h, 1 - self.p["c"]), self.other.at[k, h], "core")
                self.locals[i] = pltpu.make_async_copy(
                    self.block(k, h, self.p["c"]), self.own.at[k, h], self.local.at[i]
                )
                self.locals[i].start()

    def paired(self, k):
        up, down = self.first + "_up", self.first + "_down"
        for h in range(2):
            i = 2 * k + h
            self.copies[CORE + i].wait_recv()
            self.locals[i].wait()

            def body(s, carry, h=h):
                self.own[k, h, s] = self.own[k, h, s] + self.other[k, h, s]
                return carry

            lax.fori_loop(0, 4, body, 0)
            block = self.own.at[k, h]
            if k == 2:
                self.go(VIA + h, block, self.via.at[h], (up, down)[h])
            elif k == 1 and h == 1:
                self.go(DIRECT + 1, block, self.fin.at[0, 1], up)
            elif k == 3 and h == 0:
                self.go(DIRECT + 2, block, self.fin.at[1, 0], down)

    def relayed(self):
        for h, k, to, i in ((0, 1, "_up", DIRECT), (1, 3, "_down", DIRECT + 3)):
            self.copies[VIA + h].wait_recv()

            def body(s, carry, h=h, k=k):
                self.own[k, h, s] = self.own[k, h, s] + self.via[h, s]
                return carry

            lax.fori_loop(0, 4, body, 0)
            self.go(i, self.own.at[k, h], self.fin.at[h, h], self.first + to)

    def first_done(self):
        m = self.p[self.second]
        up, down = self.second + "_up", self.second + "_down"
        for i in range(4):
            self.copies[DIRECT + i].wait_recv()
        for k in ORDER:
            at = (m + k) % 4
            for h in range(2):
                self.own[0, h, at] = self.own[0, h, at] + self.fin[0, h, at] + self.fin[1, h, at]
                block = self.own.at[0, h, at]
                if k == 2:
                    self.go(VIA2 + h, block, self.via2.at[h], (up, down)[h])
                elif k == 1 and h == 1:
                    self.go(DIRECT2 + 1, block, self.fin2.at[0, 1], up)
                elif k == 3 and h == 0:
                    self.go(DIRECT2 + 2, block, self.fin2.at[1, 0], down)

    def relayed2(self):
        m = self.p[self.second]
        for h, k, to, i in ((0, 1, "_up", DIRECT2), (1, 3, "_down", DIRECT2 + 3)):
            at = (m + k) % 4
            self.copies[VIA2 + h].wait_recv()
            self.own[0, h, at] = self.own[0, h, at] + self.via2[h]
            self.go(i, self.own.at[0, h, at], self.fin2.at[h, h], self.second + to)

    def second_done(self):
        m, x = self.p[self.second], self.p["x"]
        for i in range(4):
            self.copies[DIRECT2 + i].wait_recv()
        for h in range(2):
            self.own[0, h, m] = self.own[0, h, m] + self.fin2[0, h] + self.fin2[1, h]
        self.go(LAST, self.own.at[0, 1 - x, m], self.last, "x")

    def finish(self):
        m, x = self.p[self.second], self.p["x"]
        self.copies[LAST].wait_recv()
        self.out[...] = self.own[0, x, m] + self.last[...]
        for copy in self.copies.values():
            copy.wait_send()


SCATTER_REFS = len(scatter_scratch(128))


def small_scratch(rows, both):
    return [
        pltpu.VMEM((both, 128), jnp.float32),
        pltpu.VMEM((2, rows, 128), jnp.float32),
        pltpu.VMEM((2, rows, 128), jnp.float32),
        pltpu.VMEM((4, rows, 128), jnp.float32),
        pltpu.VMEM((4, rows, 128), jnp.float32),
        pltpu.SemaphoreType.DMA((2, 9)),
    ]


SMALL_REFS = len(small_scratch(8, 8))


class SmallSums:
    def __init__(self, rows, out, p, near, scratch):
        self.rows, self.out, self.p, self.near = rows, out, p, near
        self.from_partner, self.held, self.pair, self.along_y, self.along_z, self.sems = scratch
        self.both = self.from_partner.shape[0]
        self.copies = []

    def go(self, i, src, dst, to):
        copy = remote(src, dst, self.sems, i, self.near[to])
        copy.start()
        self.copies.append(copy)

    def start(self):
        self.go(0, self.rows.at[pl.ds(0, self.both)], self.from_partner, "partner")

    def to_core(self):
        self.copies[0].wait_recv()
        self.held[0] = self.rows[...]
        self.held[0, pl.ds(0, self.both)] = self.rows[pl.ds(0, self.both)] + self.from_partner[...]
        self.go(1, self.held.at[0], self.pair.at[0], "core")

    def ring(self, axis, line, first):
        for i, name in enumerate(("_up", "_far", "_down")):
            self.go(first + i, line.at[self.p[axis]], line.at[self.p[axis]], axis + name)

    def to_y(self):
        self.copies[1].wait_recv()
        self.along_y[self.p["y"]] = self.held[0] + self.pair[0]
        self.ring("y", self.along_y, 2)

    def to_z(self):
        for i in range(2, 5):
            self.copies[i].wait_recv()
        a = self.along_y
        self.along_z[self.p["z"]] = a[0] + a[1] + a[2] + a[3]
        self.ring("z", self.along_z, 5)

    def to_x(self):
        for i in range(5, 8):
            self.copies[i].wait_recv()
        a = self.along_z
        self.held[1] = a[0] + a[1] + a[2] + a[3]
        self.go(8, self.held.at[1], self.pair.at[1], "x")

    def finish(self):
        self.copies[8].wait_recv()
        self.out[...] = self.held[1] + self.pair[1]
        for copy in self.copies:
            copy.wait_send()


def reduce_kernel(firsts, has_small, *refs):
    refs = list(refs)

    def take(count):
        taken, refs[:] = refs[:count], refs[count:]
        return taken

    (terms_ref,), grads = take(1), take(len(firsts))
    rows = take(1) if has_small else []
    (theirs_ref,), outs = take(1), take(len(firsts))
    sums = take(1) if has_small else []
    p = place()
    near = neighbours(p)
    swap_sems = take(1)[0]
    scatters = [Scatter(g, o, f, p, near, take(SCATTER_REFS)) for g, o, f in zip(grads, outs, firsts)]
    small = SmallSums(rows[0], sums[0], p, near, take(SMALL_REFS)) if has_small else None
    names = ["partner", "core", "x", "y_up", "y_down", "z_up", "z_down"]
    if has_small:
        names += ["y_far", "z_far"]
    greet([near[name] for name in names])
    if has_small:
        small.start()
    swap = remote(terms_ref, theirs_ref, swap_sems, 0, near["partner"])
    swap.start()
    for s in scatters:
        s.start()
    beside = ["to_core", "to_y", "to_z", "to_x"]
    for k in ORDER:
        for s in scatters:
            s.paired(k)
        if has_small:
            getattr(small, beside.pop(0))()
    for name in ("relayed", "first_done", "relayed2", "second_done", "finish"):
        for s in scatters:
            getattr(s, name)()
    if has_small:
        small.finish()
    swap.wait()


def exchange_and_reduce(terms, grads, firsts, collective_id, rows=None, both=0):
    f32 = jnp.float32
    args = [terms] + [g.reshape(4, 2, 4, 2, 16, g.shape[1]) for g in grads]
    in_specs = [IN_PLACE] * len(args)
    out_shape = [jax.ShapeDtypeStruct(terms.shape, f32)]
    out_shape += [jax.ShapeDtypeStruct((16, g.shape[1]), f32) for g in grads]
    out_specs = [IN_PLACE] + [IN_VMEM] * len(grads)
    scratch = [pltpu.SemaphoreType.DMA((2, 1))]
    for g in grads:
        scratch += scatter_scratch(g.shape[1])
    if rows is not None:
        args.append(rows)
        in_specs.append(IN_VMEM)
        out_shape.append(jax.ShapeDtypeStruct(rows.shape, f32))
        out_specs.append(IN_VMEM)
        scratch += small_scratch(rows.shape[0], both)
    return pl.pallas_call(
        functools.partial(reduce_kernel, firsts, rows is not None),
        out_shape=out_shape,
        in_specs=in_specs,
        out_specs=out_specs,
        scratch_shapes=scratch,
        compiler_params=pltpu.CompilerParams(
            collective_id=collective_id, has_side_effects=True, vmem_limit_bytes=60 * 1024 * 1024
        ),
    )(*args)


def from_partner(value):
    return lax.ppermute(value, "tensor", [(0, 1), (1, 0)])


def layer_norm(values, gain, shift):
    centre = values - jnp.mean(values, axis=-1, keepdims=True)
    inverse = lax.rsqrt(jnp.mean(centre * centre, axis=-1, keepdims=True) + EPS)
    normed = centre * inverse
    return (normed * gain + shift, normed, inverse)


def norm_backward(grad_out, normed, inverse, gain):
    scaled = grad_out * gain
    return inverse * (
        scaled
        - jnp.mean(scaled, axis=-1, keepdims=True)
        - normed * jnp.mean(scaled * normed, axis=-1, keepdims=True)
    )


def gelu_parts(inner):
    tangent = jnp.tanh(GELU_C * (inner + CUBIC * inner * inner * inner))
    value = 0.5 * inner * (1.0 + tangent)
    slope = 0.5 * (1.0 + tangent) + 0.5 * inner * (1.0 - tangent * tangent) * GELU_C * (
        1.0 + 3.0 * CUBIC * inner * inner
    )
    return (value, slope)


def fdot(left, right):
    return jnp.dot(left, right, preferred_element_type=jnp.float32)


def contract_rows(left, right):
    return jnp.einsum("ta,tb->ab", left, right, preferred_element_type=jnp.float32)


def contract_cols(left, right):
    return jnp.einsum("ta,ba->tb", left, right, preferred_element_type=jnp.float32)


BLOCK = 256
SCALE = 1.0 / HEAD_DIM**0.5


def dot_over(left, right, left_dim, right_dim):
    return lax.dot_general(
        left, right, (((left_dim,), (right_dim,)), ((), ())), preferred_element_type=jnp.float32
    )


def mask_tokens(column_ref, row_ref, mask_ref):
    u = lax.broadcasted_iota(jnp.int32, (SEQ, SEQ), 0)
    t = lax.broadcasted_iota(jnp.int32, (SEQ, SEQ), 1)
    allowed = (column_ref[...] == row_ref[...]) & (u <= t)
    mask_ref[...] = jnp.where(allowed, 0.0, -1e30)


def blocks_of_tokens():
    for at in range(0, SEQ, BLOCK):
        yield slice(at, at + BLOCK), at + BLOCK


def attend_kernel(q_ref, k_ref, v_ref, column_ref, row_ref, out_ref, log_ref, mask_ref):
    mask_tokens(column_ref, row_ref, mask_ref)

    def two_heads(i, carry):
        cols = pl.ds(pl.multiple_of(i * 2 * HEAD_DIM, 2 * HEAD_DIM), 2 * HEAD_DIM)
        halves = []
        for h in range(2):
            e = slice(h * HEAD_DIM, (h + 1) * HEAD_DIM)
            q, k, v = q_ref[:, cols][:, e], k_ref[:, cols][:, e], v_ref[:, cols][:, e]
            rows, logs = [], []
            for t, end in blocks_of_tokens():
                scores = dot_over(k[:end], q[t], 1, 1) + mask_ref[:end, t]
                top = jnp.max(scores, axis=0, keepdims=True)
                weights = jnp.exp(scores - top)
                total = jnp.sum(weights, axis=0, keepdims=True)
                probs = (weights * (1.0 / total)).astype(jnp.bfloat16)
                logs.append(top + jnp.log(total))
                rows.append(dot_over(v[:end], probs, 0, 0).T)
            log_ref[pl.ds(2 * i + h, 1), :] = jnp.concatenate(logs, axis=1)
            halves.append(jnp.concatenate(rows, axis=0))
        out_ref[:, cols] = jnp.concatenate(halves, axis=1).astype(jnp.bfloat16)
        return carry

    lax.fori_loop(0, q_ref.shape[1] // (2 * HEAD_DIM), two_heads, 0)


def attend_forward(query, keys, values, column, row):
    heads = query.shape[1] // HEAD_DIM
    return pl.pallas_call(
        attend_kernel,
        out_shape=[
            jax.ShapeDtypeStruct(query.shape, jnp.bfloat16),
            jax.ShapeDtypeStruct((heads, SEQ), jnp.float32),
        ],
        in_specs=[IN_VMEM] * 5,
        out_specs=[IN_VMEM] * 2,
        scratch_shapes=[pltpu.VMEM((SEQ, SEQ), jnp.float32)],
        compiler_params=pltpu.CompilerParams(vmem_limit_bytes=32 * 1024 * 1024),
    )(query, keys, values, column, row)


def attend_back_kernel(
    terms_ref, q_ref, k_ref, v_ref, grad_ref, log_ref, column_ref, row_ref,
    theirs_ref, gq_ref, gk_ref, gv_ref, bq_ref, bv_ref,
    mask_ref, sems,
):
    partner = neighbours(place())["partner"]
    greet([partner])
    swap = remote(terms_ref, theirs_ref, sems, 0, partner)
    swap.start()
    mask_tokens(column_ref, row_ref, mask_ref)

    def two_heads(i, carry):
        cols = pl.ds(pl.multiple_of(i * 2 * HEAD_DIM, 2 * HEAD_DIM), 2 * HEAD_DIM)
        halves = []
        for h in range(2):
            e = slice(h * HEAD_DIM, (h + 1) * HEAD_DIM)
            q, k, v, g = q_ref[:, cols][:, e], k_ref[:, cols][:, e], v_ref[:, cols][:, e], grad_ref[:, cols][:, e]
            logs = log_ref[pl.ds(2 * i + h, 1), :]
            gq, gk, gv = [], None, None
            for t, end in blocks_of_tokens():
                scores = dot_over(k[:end], q[t], 1, 1) + mask_ref[:end, t]
                probs = jnp.exp(scores - logs[:, t])
                grad_probs = dot_over(v[:end], g[t], 1, 1)
                delta = jnp.sum(probs * grad_probs, axis=0, keepdims=True)
                grad_scores = (probs * (grad_probs - delta)).astype(jnp.bfloat16)
                of_k = dot_over(grad_scores, q[t], 1, 0)
                of_v = dot_over(probs.astype(jnp.bfloat16), g[t], 1, 0)
                gq.append(dot_over(k[:end], grad_scores, 0, 0).T * SCALE)
                if gk is not None:
                    of_k = jnp.concatenate([gk + of_k[: gk.shape[0]], of_k[gk.shape[0] :]], axis=0)
                    of_v = jnp.concatenate([gv + of_v[: gv.shape[0]], of_v[gv.shape[0] :]], axis=0)
                gk, gv = of_k, of_v
            halves.append((jnp.concatenate(gq, axis=0), gk, gv))
        gq, gk, gv = (jnp.concatenate(pair, axis=1) for pair in zip(*halves))
        bq_ref[:, cols] = jnp.sum(gq, axis=0, keepdims=True)
        bv_ref[:, cols] = jnp.sum(gv, axis=0, keepdims=True)
        gq_ref[:, cols] = gq.astype(jnp.bfloat16)
        gk_ref[:, cols] = gk.astype(jnp.bfloat16)
        gv_ref[:, cols] = gv.astype(jnp.bfloat16)
        return carry

    lax.fori_loop(0, q_ref.shape[1] // (2 * HEAD_DIM), two_heads, 0)
    swap.wait()


def attend_backward(terms, query, keys, values, grad_attended, logs, column, row, collective_id):
    grad = jax.ShapeDtypeStruct(query.shape, jnp.bfloat16)
    total = jax.ShapeDtypeStruct((1, query.shape[1]), jnp.float32)
    return pl.pallas_call(
        attend_back_kernel,
        out_shape=[jax.ShapeDtypeStruct(terms.shape, jnp.float32), grad, grad, grad, total, total],
        in_specs=[IN_PLACE] + [IN_VMEM] * 7,
        out_specs=[IN_PLACE] + [IN_VMEM] * 5,
        scratch_shapes=[pltpu.VMEM((SEQ, SEQ), jnp.float32), pltpu.SemaphoreType.DMA((2, 1))],
        compiler_params=pltpu.CompilerParams(
            collective_id=collective_id, has_side_effects=True, vmem_limit_bytes=32 * 1024 * 1024
        ),
    )(terms, query, keys, values, grad_attended, logs, column, row)


def on_device(
    hidden_in,
    segment_ids,
    ln_one_gain,
    ln_one_bias,
    w_query,
    w_key,
    w_value,
    b_query,
    b_value,
    w_out,
    b_out,
    ln_two_gain,
    ln_two_bias,
    w_fc,
    b_fc,
    w_proj,
    b_proj,
    cotangent,
):
    column, row = segment_ids.reshape(SEQ, 1), segment_ids.reshape(1, SEQ)
    inputs = hidden_in.astype(jnp.float32)
    first_f, normed_one, inverse_one = layer_norm(inputs, ln_one_gain, ln_one_bias)
    first_in = first_f.astype(jnp.bfloat16)
    query = (fdot(first_in, w_query) + b_query).astype(jnp.bfloat16) * jnp.bfloat16(SCALE)
    keys = fdot(first_in, w_key).astype(jnp.bfloat16)
    values = (fdot(first_in, w_value) + b_value).astype(jnp.bfloat16)
    attended, logs = attend_forward(query, keys, values, column, row)
    attn_terms = fdot(attended, w_out)
    middle = inputs + (attn_terms + from_partner(attn_terms)) + b_out
    second_f, normed_two, inverse_two = layer_norm(middle, ln_two_gain, ln_two_bias)
    second_in = second_f.astype(jnp.bfloat16)
    inner = fdot(second_in, w_fc) + b_fc
    activated_f, slope = gelu_parts(inner)
    activated = activated_f.astype(jnp.bfloat16)
    top_grad = cotangent.astype(jnp.bfloat16)
    grad_b_proj = jnp.sum(cotangent, axis=0)
    grad_inner = contract_cols(top_grad, w_proj) * slope
    grad_b_fc = jnp.sum(grad_inner, axis=0)
    grad_inner_b = grad_inner.astype(jnp.bfloat16)
    grad_proj = contract_rows(top_grad, activated)
    grad_fc = contract_rows(second_in, grad_inner_b)
    second_terms = contract_cols(grad_inner_b, w_fc)
    second_theirs, proj_share, fc_share = exchange_and_reduce(
        second_terms, (grad_proj, grad_fc), ("y", "z"), 1
    )
    grad_second = second_terms + second_theirs
    rows_two = norm_backward(grad_second, normed_two, inverse_two, ln_two_gain)
    grad_ln_two_gain = jnp.sum(grad_second * normed_two, axis=0)
    grad_ln_two_bias = jnp.sum(grad_second, axis=0)
    grad_middle = cotangent + rows_two
    grad_b_out = jnp.sum(grad_middle, axis=0)
    middle_b = grad_middle.astype(jnp.bfloat16)
    grad_w_out = contract_rows(middle_b, attended)
    grad_attended = contract_cols(middle_b, w_out).astype(jnp.bfloat16)
    mlp_terms = fdot(activated, w_proj)
    mlp_theirs, grad_q_b, grad_k_b, grad_v_b, grad_b_query, grad_b_value = attend_backward(
        mlp_terms, query, keys, values, grad_attended, logs, column, row, 3
    )
    block_out = middle + (mlp_terms + mlp_theirs) + b_proj
    grad_query = contract_rows(first_in, grad_q_b)
    grad_key = contract_rows(first_in, grad_k_b)
    grad_value = contract_rows(first_in, grad_v_b)
    first_terms = (
        contract_cols(grad_q_b, w_query)
        + contract_cols(grad_k_b, w_key)
        + contract_cols(grad_v_b, w_value)
    )
    small = (
        jnp.sum(first_terms * normed_one, axis=0),
        jnp.sum(first_terms, axis=0),
        grad_b_query,
        grad_b_value,
        grad_b_out,
        grad_ln_two_gain,
        grad_ln_two_bias,
        grad_b_fc,
        grad_b_proj,
    )
    rows = jnp.concatenate([part.reshape(-1, 128) for part in small], axis=0)
    both = (small[0].size + small[1].size) // 128
    first_theirs, query_share, key_share, value_share, out_share, sums = exchange_and_reduce(
        first_terms, (grad_query, grad_key, grad_value, grad_w_out), ("y", "y", "z", "z"), 2, rows, both
    )
    input_grad = grad_middle + norm_backward(first_terms + first_theirs, normed_one, inverse_one, ln_one_gain)
    totals, at = [], 0
    for part in small:
        count = part.size // 128
        totals.append(sums[at : at + count].reshape(-1))
        at += count
    return (
        block_out,
        input_grad,
        totals[0],
        totals[1],
        query_share,
        key_share,
        value_share,
        totals[2],
        totals[3],
        out_share.T,
        totals[4],
        totals[5],
        totals[6],
        fc_share,
        totals[7],
        proj_share.T,
        totals[8],
    )


def solution(mesh):
    in_specs = (
        P("dp", None),
        P("dp"),
        P(),
        P(),
        P(None, "tensor"),
        P(None, "tensor"),
        P(None, "tensor"),
        P("tensor"),
        P("tensor"),
        P("tensor", None),
        P(),
        P(),
        P(),
        P(None, "tensor"),
        P("tensor"),
        P("tensor", None),
        P(),
        P("dp", None),
    )
    out_specs = (
        P("dp", None),
        P("dp", None),
        P(),
        P(),
        P("dp", "tensor"),
        P("dp", "tensor"),
        P("dp", "tensor"),
        P("tensor"),
        P("tensor"),
        P("tensor", "dp"),
        P(),
        P(),
        P(),
        P("dp", "tensor"),
        P("tensor"),
        P("tensor", "dp"),
        P(),
    )
    return jax.shard_map(
        on_device, mesh=mesh, in_specs=in_specs, out_specs=out_specs, check_vma=False
    )
```
